32 devices in a mesh: seq: 8 (over z, y), mp: 4 (over x, core).
Axes of the slice: x: 2, y: 2, z: 4, core: 2. Of those that a mesh axis runs over, the one named last changes fastest.
Arguments:
- incoming_image_patches: bfloat16 [1, 128, 128, 1152], P(None, 'seq', 'mp'), may hold values from -6 to 6
- initial_standardize_scaling: float32 [1152], replicated, may hold values from 0.1 to 1.9
- acceptance_matrix: bfloat16 [1152, 1024], P(None, 'mp'), may hold values from -0.1875 to 0.1875
- addressing_matrix: bfloat16 [1152, 1024], P(None, 'mp'), may hold values from -0.1875 to 0.1875
- content_matrix: bfloat16 [1152, 1024], P(None, 'mp'), may hold values from -0.1875 to 0.1875
- forgetting_lowdim_left_factor: bfloat16 [1152, 64], replicated, may hold values from -0.1875 to 0.1875
- forgetting_lowdim_right_factor: bfloat16 [64, 1024], P(None, 'mp'), may hold values from -1.5 to 1.5
- forgetting_baseline: float32 [1024], P('mp'), may hold values from -6 to 1
- self_token_reward: float32 [1024], P('mp'), may hold values from -3 to 3
- horizontal_cluster_scaling: float32 [1024], P('mp'), may hold values from 0.1 to 1.9
- vertical_cluster_scaling: float32 [1024], P('mp'), may hold values from 0.1 to 1.9
- temporal_mix_projection_matrix: bfloat16 [1024, 1152], P('mp'), may hold values from -0.1875 to 0.1875
- later_standardize_scaling: float32 [1152], replicated, may hold values from 0.1 to 1.9
- feature_mix_addressing_matrix: bfloat16 [1152, 4608], P('seq', 'mp'), may hold values from -0.1875 to 0.1875
- feature_mix_content_matrix: bfloat16 [4608, 1152], P('mp', 'seq'), may hold values from -0.09375 to 0.09375
Outputs:
- block_out: bfloat16 [1, 128, 128, 1152], P(None, 'seq', 'mp')
The draws below stay inside these ranges and needn't reach their ends.
All inputs are finite; a program needn't handle non-finite values.
Results may differ from the reference program's by a relative error of at most 0.017.
Values may be sent and summed in bfloat16 or wider, within the bound.
A program may use at most 128 MiB of HBM per device.

```python
import jax
import jax.numpy as jnp
from jax import lax

MODEL_DIM = 1152
ATTENTION_SPLITS = 16
SUBSPACE_SIZE = 64
DECAY_RANK = 64
FF = 4608
IMGS = 1
HGT = 128
WID = 128
N_MP = 4


def steps_of(stream_key, dims, shards, smallest, top_value):
    def one(dim, shards_of):
        heights = jax.random.uniform(jax.random.fold_in(jax.random.fold_in(stream_key, 6), dim), (shards_of,), jnp.float32, smallest / len(shards), top_value / len(shards))
        return jnp.repeat(jnp.exp(heights), dims[dim] // shards_of).reshape((-1,) + (1,) * (len(dims) - dim - 1))

    level = one(*shards[0])
    for cut in shards[1:]:
        level = level * one(*cut)
    return level


def bell_draw(key, dims, deviation, limit, cuts=(), dtype=jnp.bfloat16):
    entries = jax.random.normal(key, dims, jnp.float32) * deviation
    if len(cuts) > 0:
        entries = steps_of(key, dims, cuts, -0.22, 0.18) * entries
    return jnp.clip(entries, min=-limit, max=limit).astype(dtype)


def setup_inputs(seed: int = 0) -> dict:
    key_of = jax.random.split(jax.random.key(seed), 16)
    incoming_image_patches = bell_draw(key_of[0], (IMGS, HGT, WID, MODEL_DIM), 1.0, 6.0, ((1, 8), (2, 4)))
    initial_standardize_scaling = jnp.clip(1.0 + 0.18 * jax.random.normal(key_of[1], (MODEL_DIM,), jnp.float32), 0.1, 1.9)
    acceptance_matrix = bell_draw(key_of[2], (MODEL_DIM, ATTENTION_SPLITS * SUBSPACE_SIZE), MODEL_DIM ** -0.5, 0.1875, ((1, 4),))
    addressing_matrix = bell_draw(key_of[3], (MODEL_DIM, ATTENTION_SPLITS * SUBSPACE_SIZE), MODEL_DIM ** -0.5, 0.1875, ((1, 4),))
    content_matrix = bell_draw(key_of[4], (MODEL_DIM, ATTENTION_SPLITS * SUBSPACE_SIZE), MODEL_DIM ** -0.5, 0.1875, ((1, 4),))
    forgetting_lowdim_left_factor = bell_draw(key_of[5], (MODEL_DIM, DECAY_RANK), MODEL_DIM ** -0.5, 0.1875)
    forgetting_lowdim_right_factor = bell_draw(key_of[6], (DECAY_RANK, ATTENTION_SPLITS * SUBSPACE_SIZE), 0.25, 1.5, ((1, 4),))
    forgetting_baseline = jnp.clip(-6.0 + 7.0 * jax.random.uniform(key_of[7], (ATTENTION_SPLITS * SUBSPACE_SIZE,), jnp.float32) ** steps_of(key_of[7], (ATTENTION_SPLITS * SUBSPACE_SIZE,), ((0, 4),), -0.2, 0.2), -6.0, 1.0)
    self_token_reward = bell_draw(key_of[8], (ATTENTION_SPLITS * SUBSPACE_SIZE,), 0.5, 3.0, ((0, 4),), jnp.float32)
    horizontal_cluster_scaling = jnp.clip(1.0 + 0.18 * jax.random.normal(key_of[9], (ATTENTION_SPLITS * SUBSPACE_SIZE,), jnp.float32), 0.1, 1.9)
    vertical_cluster_scaling = jnp.clip(1.0 + 0.18 * jax.random.normal(key_of[10], (ATTENTION_SPLITS * SUBSPACE_SIZE,), jnp.float32), 0.1, 1.9)
    temporal_mix_projection_matrix = bell_draw(key_of[11], (ATTENTION_SPLITS * SUBSPACE_SIZE, MODEL_DIM), (ATTENTION_SPLITS * SUBSPACE_SIZE) ** -0.5, 0.1875, ((0, 4),))
    later_standardize_scaling = jnp.clip(1.0 + 0.18 * jax.random.normal(key_of[12], (MODEL_DIM,), jnp.float32), 0.1, 1.9)
    feature_mix_addressing_matrix = bell_draw(key_of[13], (MODEL_DIM, FF), MODEL_DIM ** -0.5, 0.1875, ((0, 8), (1, 4)))
    feature_mix_content_matrix = bell_draw(key_of[14], (FF, MODEL_DIM), FF ** -0.5, 0.09375, ((0, 4), (1, 8)))
    return dict(incoming_image_patches=incoming_image_patches, initial_standardize_scaling=initial_standardize_scaling, acceptance_matrix=acceptance_matrix, addressing_matrix=addressing_matrix, content_matrix=content_matrix, forgetting_lowdim_left_factor=forgetting_lowdim_left_factor, forgetting_lowdim_right_factor=forgetting_lowdim_right_factor, forgetting_baseline=forgetting_baseline, self_token_reward=self_token_reward, horizontal_cluster_scaling=horizontal_cluster_scaling, vertical_cluster_scaling=vertical_cluster_scaling, temporal_mix_projection_matrix=temporal_mix_projection_matrix, later_standardize_scaling=later_standardize_scaling, feature_mix_addressing_matrix=feature_mix_addressing_matrix, feature_mix_content_matrix=feature_mix_content_matrix)


def layer_norm(inputs, gain):
    values = inputs.astype(jnp.float32)
    average = lax.optimization_barrier(jnp.mean(values, axis=-1, keepdims=True))
    centred = values - average
    spread = lax.optimization_barrier(jnp.mean(centred * centred, axis=-1, keepdims=True))
    return (centred * lax.rsqrt(spread + 1e-05) * gain).astype(jnp.bfloat16)

def heads_first(array, nheads):
    number, length, inner_width = array.shape
    shaped = array.astype(jnp.float32).reshape(number, length, nheads, inner_width // nheads)
    return shaped.transpose(0, 2, 1, 3)

def recurrence(recept_in, keying_in, decays_in, valued_in, boost_in, gain):
    number, length, inner_width = recept_in.shape
    nheads = inner_width // SUBSPACE_SIZE
    head_size = inner_width // nheads
    blocks = length // 16
    acceptance_horizontal_lines = heads_first(recept_in, nheads)
    addressing_horizontal_lines = heads_first(keying_in, nheads)
    decays = heads_first(decays_in, nheads)
    content_horizontal_lines = heads_first(valued_in, nheads)
    boost = boost_in.reshape(nheads, 1, head_size)
    running = jnp.cumsum(decays, axis=2)
    before = running - decays
    before_blocks = before.reshape(number, nheads, blocks, 16, head_size)
    anchor = before_blocks[:, :, :, :1, :]
    queries = acceptance_horizontal_lines.reshape(number, nheads, blocks, 16, head_size) * jnp.exp(before_blocks - anchor)
    places = jnp.arange(length)
    limits = (jnp.arange(blocks) + 1) * 16
    usable = places[None, :] < limits[:, None]
    exponent = anchor - running[:, :, None, :, :]
    exponent = jnp.where(usable[None, None, :, :, None], exponent, -10000.0)
    weighted = addressing_horizontal_lines[:, :, None, :, :] * jnp.exp(exponent)
    scores = jnp.einsum('nhbqc,nhbsc->nhbqs', queries, weighted, precision=lax.Precision.HIGHEST)
    query_places = places.reshape(blocks, 16)
    earlier = places[None, None, :] < query_places[:, :, None]
    scores = jnp.where(earlier[None, None], scores, 0.0)
    current = lax.optimization_barrier(jnp.sum(acceptance_horizontal_lines * boost * addressing_horizontal_lines, axis=-1))
    summed = jnp.einsum('nhbqs,nhsc->nhbqc', scores, content_horizontal_lines, precision=lax.Precision.HIGHEST)
    summed = summed.reshape(number, nheads, length, head_size) + current[..., None] * content_horizontal_lines
    average = lax.optimization_barrier(jnp.mean(summed, axis=-1, keepdims=True))
    centred = summed - average
    spread = lax.optimization_barrier(jnp.mean(centred * centred, axis=-1, keepdims=True))
    normed = (centred * lax.rsqrt(spread + 0.00064)).transpose(0, 2, 1, 3).reshape(number, length, inner_width)
    return (normed * gain).astype(jnp.bfloat16)

def single_strip_sweep(arrays, boost, gain):

    def single(items):
        return recurrence(items[0][None], items[1][None], items[2][None], items[3][None], boost, gain)[0]
    return lax.map(single, arrays)

def reference(incoming_image_patches, initial_standardize_scaling, acceptance_matrix, addressing_matrix, content_matrix, forgetting_lowdim_left_factor, forgetting_lowdim_right_factor, forgetting_baseline, self_token_reward, horizontal_cluster_scaling, vertical_cluster_scaling, temporal_mix_projection_matrix, later_standardize_scaling, feature_mix_addressing_matrix, feature_mix_content_matrix):
    inner_width = ATTENTION_SPLITS * SUBSPACE_SIZE
    xn1 = layer_norm(incoming_image_patches, initial_standardize_scaling).reshape(-1, MODEL_DIM)
    acceptance_horizontal_lines = jnp.dot(xn1, acceptance_matrix, preferred_element_type=jnp.float32).astype(jnp.bfloat16)
    addressing_horizontal_lines = jnp.dot(xn1, addressing_matrix, preferred_element_type=jnp.float32).astype(jnp.bfloat16)
    content_horizontal_lines = jnp.dot(xn1, content_matrix, preferred_element_type=jnp.float32).astype(jnp.bfloat16)
    latent = jnp.tanh(jnp.dot(xn1, forgetting_lowdim_left_factor, preferred_element_type=jnp.float32)).astype(jnp.bfloat16)
    forgetting_log_amount = (-0.7 * jax.nn.sigmoid(forgetting_baseline + jnp.dot(latent, forgetting_lowdim_right_factor, preferred_element_type=jnp.float32))).astype(jnp.bfloat16)

    def horizontal_sweep(array):
        return array.reshape(IMGS * HGT, WID, inner_width)

    def vertical_sweep(array):
        return array.reshape(IMGS, HGT, WID, inner_width).transpose(0, 2, 1, 3).reshape(IMGS * WID, HGT, inner_width)
    horizontal_recurrence_result = single_strip_sweep((horizontal_sweep(acceptance_horizontal_lines), horizontal_sweep(addressing_horizontal_lines), horizontal_sweep(forgetting_log_amount), horizontal_sweep(content_horizontal_lines)), self_token_reward, horizontal_cluster_scaling)
    vertical_recurrence_result = single_strip_sweep((vertical_sweep(acceptance_horizontal_lines), vertical_sweep(addressing_horizontal_lines), vertical_sweep(forgetting_log_amount), vertical_sweep(horizontal_recurrence_result)), self_token_reward, vertical_cluster_scaling)
    vertical_recurrence_result = vertical_recurrence_result.reshape(IMGS, WID, HGT, inner_width).transpose(0, 2, 1, 3).reshape(-1, inner_width)
    group = inner_width // N_MP
    attended = jnp.zeros((IMGS * HGT * WID, MODEL_DIM), jnp.float32)
    for index in range(N_MP):
        partial_value = jnp.dot(vertical_recurrence_result[:, index * group:(index + 1) * group], temporal_mix_projection_matrix[index * group:(index + 1) * group], preferred_element_type=jnp.float32)
        attended = attended + lax.optimization_barrier(partial_value.astype(jnp.bfloat16)).astype(jnp.float32)
    residual = (incoming_image_patches.reshape(-1, MODEL_DIM).astype(jnp.float32) + attended).astype(jnp.bfloat16)
    xn2 = layer_norm(residual, later_standardize_scaling)
    units = FF // N_MP
    mixed = jnp.zeros((IMGS * HGT * WID, MODEL_DIM), jnp.float32)
    for index in range(N_MP):
        hidden_pre = jnp.dot(xn2, feature_mix_addressing_matrix[:, index * units:(index + 1) * units], preferred_element_type=jnp.float32)
        positive = jnp.maximum(hidden_pre, 0.0)
        hidden = (positive * positive).astype(jnp.bfloat16)
        partial_value = jnp.dot(hidden, feature_mix_content_matrix[index * units:(index + 1) * units], preferred_element_type=jnp.float32)
        mixed = mixed + lax.optimization_barrier(partial_value.astype(jnp.bfloat16)).astype(jnp.float32)
    block_out = (residual.astype(jnp.float32) + mixed).astype(jnp.bfloat16)
    return block_out.reshape(IMGS, HGT, WID, MODEL_DIM)
```

```python
import functools
import math

import jax
import jax.numpy as jnp
from jax import lax
from jax.experimental import pallas as pl
from jax.sharding import Mesh, PartitionSpec as P

SUBSPACE_SIZE = 64
MP = ("mx", "mc")


def layer_norm(inputs, gain):
    values = inputs.astype(jnp.float32)
    average = jnp.mean(values, axis=-1, keepdims=True)
    centred = values - average
    spread = jnp.mean(centred * centred, axis=-1, keepdims=True)
    return (centred * lax.rsqrt(spread + 1e-05) * gain).astype(jnp.bfloat16)


def split_dot(a, b):
    high = a.astype(jnp.bfloat16)
    low = (a - high.astype(jnp.float32)).astype(jnp.bfloat16)
    return jnp.dot(high, b, preferred_element_type=jnp.float32) + jnp.dot(
        low, b, preferred_element_type=jnp.float32
    )


def recurrence_kernel(
    lines, width, rkl_ref, v_ref, right_ref, base_ref, bonus_ref, gain_ref, tri_ref, same_ref, out_ref
):
    length = rkl_ref.shape[1]
    nheads = width // SUBSPACE_SIZE
    lane_head = lax.broadcasted_iota(jnp.int32, (1, width), 1) // SUBSPACE_SIZE
    earlier = lax.broadcasted_iota(jnp.int32, (length, length), 0) > lax.broadcasted_iota(
        jnp.int32, (length, length), 1
    )
    tri = tri_ref[...]
    same = same_ref[...]
    for line in range(lines):
        recept = rkl_ref[line, :, :width].astype(jnp.float32)
        keying = rkl_ref[line, :, width : 2 * width].astype(jnp.float32)
        latent = rkl_ref[line, :, 2 * width :]
        valued = v_ref[line]
        decay = (
            -0.7
            * jax.nn.sigmoid(
                base_ref[...] + jnp.dot(latent, right_ref[...], preferred_element_type=jnp.float32)
            )
        ).astype(jnp.bfloat16)
        running = jnp.dot(tri, decay, preferred_element_type=jnp.float32)
        middle = length // 2
        shifted = running - running[middle : middle + 1, :]
        queries = (recept * jnp.exp(shifted - decay.astype(jnp.float32))).astype(jnp.bfloat16)
        weighted = (keying * jnp.exp(-shifted)).astype(jnp.bfloat16)
        zero = jnp.zeros_like(queries)
        stacked = jnp.concatenate(
            [jnp.where(lane_head == head, queries, zero) for head in range(nheads)], axis=0
        )
        scores = lax.dot_general(
            stacked, weighted, (((1,), (1,)), ((), ())), preferred_element_type=jnp.float32
        )
        current = split_dot(recept * bonus_ref[...] * keying, same) * float(SUBSPACE_SIZE)
        summed = current * valued.astype(jnp.float32)
        for head in range(nheads):
            part = jnp.where(earlier, scores[head * length : (head + 1) * length], 0.0)
            product = jnp.dot(part.astype(jnp.bfloat16), valued, preferred_element_type=jnp.float32)
            summed = summed + jnp.where(lane_head == head, product, 0.0)
        centred = summed - split_dot(summed, same)
        spread = jnp.dot(
            (centred * centred).astype(jnp.bfloat16), same, preferred_element_type=jnp.float32
        )
        out_ref[line] = (centred * lax.rsqrt(spread + 0.00064) * gain_ref[...]).astype(jnp.bfloat16)


def recurrence(rkl, valued, right, base, bonus, gain, lines):
    number, length, width = valued.shape
    rank = right.shape[0]
    lines = math.gcd(lines, number)
    places = jnp.arange(length)
    tri = (places[:, None] >= places[None, :]).astype(jnp.bfloat16)
    heads = jnp.arange(width) // SUBSPACE_SIZE
    same = (heads[:, None] == heads[None, :]).astype(jnp.bfloat16) / SUBSPACE_SIZE
    fixed = lambda shape: pl.BlockSpec(shape, lambda i: (0, 0))
    wide = rkl.shape[2]
    return pl.pallas_call(
        functools.partial(recurrence_kernel, lines, width),
        grid=(number // lines,),
        in_specs=[
            pl.BlockSpec((lines, length, wide), lambda i: (i, 0, 0)),
            pl.BlockSpec((lines, length, width), lambda i: (i, 0, 0)),
            fixed((rank, width)),
            fixed((1, width)),
            fixed((1, width)),
            fixed((1, width)),
            fixed((length, length)),
            fixed((width, width)),
        ],
        out_specs=pl.BlockSpec((lines, length, width), lambda i: (i, 0, 0)),
        out_shape=jax.ShapeDtypeStruct((number, length, width), jnp.bfloat16),
        cost_estimate=pl.CostEstimate(
            flops=number * length * width * 4 * (length * 6 + width * 4),
            bytes_accessed=number * length * (wide + 2 * width) * 2,
            transcendentals=number * length * width * 3,
        ),
    )(rkl, valued, right, base[None], bonus[None], gain[None], tri, same)


def gather_columns(own):
    if lax.axis_size("mx") != 2 or lax.axis_size("mc") != 2:
        return lax.all_gather(own, MP, axis=2, tiled=True)
    swap = [(0, 1), (1, 0)]
    across = lax.ppermute(own, "mx", swap)
    beside = lax.ppermute(own, "mc", swap)
    corner = lax.ppermute(across, "mc", swap)
    first = lax.axis_index("mx") == 0
    left_core = lax.axis_index("mc") == 0
    near = (jnp.where(left_core, own, beside), jnp.where(left_core, beside, own))
    far = (jnp.where(left_core, across, corner), jnp.where(left_core, corner, across))
    return jnp.concatenate(
        [jnp.where(first, a, b) for a, b in zip(near, far)]
        + [jnp.where(first, b, a) for a, b in zip(near, far)],
        axis=2,
    )


def shards(
    incoming,
    first_gain,
    acceptance,
    addressing,
    content,
    left,
    right,
    baseline,
    reward,
    row_gain,
    col_gain,
    projection,
    later_gain,
    mix_in,
    mix_out,
):
    images, rows, _, model_width = incoming.shape
    width = acceptance.shape[1]
    halves = jnp.concatenate([mix_in, mix_out.T], axis=0)
    depth = mix_in.shape[0]
    if SPLIT == 1:
        halves = lax.all_gather(halves, "mx", axis=1, tiled=True)
    halves = lax.all_gather(halves, "seq", axis=0, tiled=False)
    if SPLIT == 2:
        halves = lax.all_gather(halves, "mx", axis=2, tiled=True)
    whole_in = halves[:, :depth].reshape(-1, halves.shape[2])
    whole_out = halves[:, depth:].reshape(-1, halves.shape[2])
    whole_projection = lax.all_gather(projection, MP, axis=0, tiled=True)
    xn1 = gather_columns(layer_norm(incoming, first_gain))
    cols = xn1.shape[2]
    tokens = xn1.reshape(-1, model_width)
    rk = jnp.dot(
        tokens, jnp.concatenate([acceptance, addressing], axis=1), preferred_element_type=jnp.float32
    ).astype(jnp.bfloat16)
    latent = jnp.tanh(jnp.dot(tokens, left, preferred_element_type=jnp.float32)).astype(jnp.bfloat16)
    valued = jnp.dot(tokens, content, preferred_element_type=jnp.float32).astype(jnp.bfloat16)
    rkl = jnp.concatenate([rk, latent], axis=1)
    wide = rkl.shape[1]

    def by_columns(array):
        last = array.shape[-1]
        turned = jnp.swapaxes(array.reshape(images, rows, cols, last), 1, 2)
        moved = lax.all_to_all(turned, "seq", split_axis=1, concat_axis=2, tiled=True)
        return moved.reshape(-1, moved.shape[2], last)

    col_rkl = by_columns(rkl)
    row_out = recurrence(
        rkl.reshape(-1, cols, wide),
        valued.reshape(-1, cols, width),
        right,
        baseline,
        reward,
        row_gain,
        2,
    )
    col_valued = by_columns(row_out)
    col_out = recurrence(col_rkl, col_valued, right, baseline, reward, col_gain, 2)
    own_cols = col_out.shape[0] // images
    col_out = col_out.reshape(images, own_cols, -1, width)
    back = lax.all_to_all(col_out, "seq", split_axis=2, concat_axis=1, tiled=True)
    mine = lax.all_to_all(back, MP, split_axis=1, concat_axis=3, tiled=True)
    mine = jnp.swapaxes(mine, 1, 2)
    attended = jnp.dot(
        mine.reshape(-1, mine.shape[3]), whole_projection, preferred_element_type=jnp.float32
    ).reshape(incoming.shape)
    residual = (incoming.astype(jnp.float32) + attended).astype(jnp.bfloat16)
    xn2 = layer_norm(residual, later_gain).reshape(-1, model_width)
    share = "mc" if SPLIT else MP
    xn2 = lax.all_gather(xn2, share, axis=0, tiled=True)
    positive = jnp.maximum(jnp.dot(xn2, whole_in, preferred_element_type=jnp.float32), 0.0)
    hidden = (positive * positive).astype(jnp.bfloat16)
    downward = lax.dot_general(
        hidden, whole_out, (((1,), (1,)), ((), ())), preferred_element_type=jnp.float32
    ).astype(jnp.bfloat16)
    mixed = lax.psum_scatter(downward, share, scatter_dimension=0, tiled=True)
    return (
        residual.astype(jnp.float32) + mixed.astype(jnp.float32).reshape(residual.shape)
    ).astype(jnp.bfloat16)


SPLIT = 2


def solution(mesh):
    seq, mp = mesh.devices.shape
    cores = math.gcd(mp, 2)
    fine = Mesh(mesh.devices.reshape(seq, mp // cores, cores), ("seq", "mx", "mc"))
    placed = (
        P(None, "seq", MP, None),
        P(),
        P(None, MP),
        P(None, MP),
        P(None, MP),
        P(),
        P(None, MP),
        P(MP),
        P(MP),
        P(MP),
        P(MP),
        P(MP, None),
        P(),
        P("seq", MP),
        P(MP, "seq"),
    )
    return jax.shard_map(
        shards, mesh=fine, in_specs=placed, out_specs=P(None, "seq", MP, None), check_vma=False
    )
```
